32 devices in a mesh: dp: 2 (over x), pipe: 4 (over z), expert: 4 (over y, core).
Axes of the slice: x: 2, y: 2, z: 4, core: 2. Of those that a mesh axis runs over, the one named last changes fastest.
Arguments:
- out_grad: bfloat16 [1024, 4096], P(('dp', 'expert'), 'pipe'), may hold values from -6 to 6
- expert_ids: int32 [1024, 2], P(('dp', 'expert')), may hold values from 0 to 3, all different within a row; in each aligned block of 128 rows (0 to 127, 128 to 255, ...) at most 80 rows name the same one
- combine_weights: float32 [1024, 2], P(('dp', 'expert')), may hold values from 0.1 to 1
- down_weight: bfloat16 [4, 7168, 4096], P('expert', 'pipe'), may hold values from -0.0625 to 0.0625
- saved_pre: bfloat16 [4, 2, 640, 7168], P('expert', None, 'dp', 'pipe'), may hold values from -6 to 6
Outputs:
- pre_grad: bfloat16 [4, 2, 640, 7168], P('expert', None, 'dp', 'pipe')
- w_grad: bfloat16 [4, 7168, 4096], P('expert', 'pipe', 'dp')
- prob_grad: float32 [1024, 2], P(('dp', 'expert'))
The draws below stay inside these ranges and needn't reach their ends.
Inputs may be any that keep to these rules, and one draw needn't show every extreme that they name: `expert_ids`: the 2 ids of a row differ. In each aligned block of 128 rows (the tokens of one device) no expert is named by more than 80 rows, a bound that some block reaches.
All inputs are finite; a program needn't handle non-finite values.
Results may differ from the reference program's by a relative error of at most 0.0064.
Values may be sent and summed in bfloat16 or wider, within the bound.
A program may use at most 128 MiB of HBM per device.

```python
import math
import jax
import jax.numpy as jnp
import numpy as np
from jax import lax

D = 4096
FF = 7168
TOP = 2
TOK_DEV = 128
EXPERTS = 4
CAP = 80
TOKENS = 1024
SLOTS = 640


def steps_of(stream_key, shape, cuts, smallest, high):
    gain = 1.0
    for axis_at, shards_of in cuts:
        steps = jax.random.uniform(jax.random.fold_in(jax.random.fold_in(stream_key, 6), axis_at), (shards_of,), jnp.float32, smallest / len(cuts), high / len(cuts))
        gain = gain * jnp.repeat(jnp.exp(steps), shape[axis_at] // shards_of).reshape((-1,) + (1,) * (len(shape) - 1 - axis_at))
    return gain


def assign_block(key, own, number, rows, number_of, top, bound, lean):
    order = jax.random.permutation(key, number_of)
    crowded, usual = load_shares(number_of, rows * top, bound, lean, True), load_shares(number_of, rows * top, bound, lean, False)
    places = jnp.arange(number_of)

    def named(tallies, rotation):
        used = int((tallies > 0).sum())
        fixed = max(1, used // 4)
        moved = fixed + (places - fixed + rotation * (used - fixed)) % max(1, number_of - fixed)
        return jnp.zeros((number_of,), jnp.int32).at[order[jnp.where(places < fixed, places, moved)]].set(jnp.asarray(tallies, jnp.int32))

    tallies = jnp.where(number % 4 == 0, named(crowded, number // 4), named(usual, number - number // 4 - 1))
    mixed = jax.random.permutation(jax.random.fold_in(own, 3), number_of)
    giver, sink = mixed[0:number_of // 2 * 2:2], mixed[1:number_of // 2 * 2:2]
    slack = jnp.minimum(tallies[giver] - 1, bound - tallies[sink]) // 2
    slack = jnp.where((giver == order[0]) | (sink == order[0]) | (tallies[sink] == 0), 0, jnp.maximum(slack, 0))
    moved = jax.random.randint(jax.random.fold_in(own, 4), (number_of // 2,), 0, 1 << 20) % (slack + 1)
    tallies = tallies.at[giver].add(-moved).at[sink].add(moved)
    members = jnp.searchsorted(jnp.cumsum(tallies), jnp.arange(rows * top), side="right").astype(jnp.int32)
    listing = members.reshape(top, rows).T
    listing = listing[jax.random.permutation(jax.random.fold_in(own, 1), rows)]
    rotation = jax.random.randint(jax.random.fold_in(own, 2), (rows, 1), 0, top)
    return jnp.take_along_axis(listing, (jnp.arange(top)[None, :] + rotation) % top, axis=1)


def load_shares(amount, total, reach, lean, full):
    weights = [(1 << 20) // math.isqrt(rank ** lean) + 1 for rank in range(1, amount + 1)]
    largest = reach if full else min(reach, max(-(-total // amount), total * weights[0] // sum(weights)))
    least = 1 if total - largest >= amount - 1 else 0
    counts, spare = [largest] + [least] * (amount - 1), total - largest - least * (amount - 1)
    while spare > 0:
        candidates = [i for i in range(1, amount) if counts[i] < largest] or [i for i in range(1, amount) if counts[i] < reach]
        mass, budget = sum([weights[i] for i in candidates]), spare
        for i in candidates:
            addition = min(reach - counts[i], max(1, budget * weights[i] // mass), spare)
            counts[i] = counts[i] + addition
            spare = spare - addition
    return np.array(counts)


def bell_draw(key, dims, deviation, most, cuts=(), kind=jnp.bfloat16):
    level = steps_of(key, dims, cuts, -0.22, 0.18) if cuts else 1.0
    array = jax.random.normal(key, dims, jnp.float32) * deviation * level
    return jnp.minimum(jnp.maximum(array, -most), most).astype(kind)


def setup_inputs(seed: int = 0) -> dict:
    key_list = jax.random.split(jax.random.key(seed), 6)
    out_grad = bell_draw(key_list[0], (TOKENS, D), 1.0, 6.0, ((0, 8), (1, 4)))
    expert_ids_keys = jax.random.split(jax.random.fold_in(key_list[1], 1), TOKENS // TOK_DEV)
    expert_ids_turns = jax.random.permutation(jax.random.fold_in(key_list[1], 3), TOKENS // TOK_DEV)
    expert_ids = jax.vmap(lambda own, number: assign_block(jax.random.fold_in(key_list[1], 2), own, number, TOK_DEV, EXPERTS, TOP, CAP, 2))(expert_ids_keys, expert_ids_turns).reshape((TOKENS, TOP))
    combine_weights = jnp.clip(0.1 + 0.9 * jax.random.uniform(key_list[2], (TOKENS, TOP), jnp.float32) ** steps_of(key_list[2], (TOKENS, TOP), ((0, 8),), -0.2, 0.2), 0.1, 1.0)
    down_weight = bell_draw(key_list[3], (EXPERTS, FF, D), FF ** -0.5, 0.0625, ((0, 4), (1, 4)))
    saved_pre = bell_draw(key_list[4], (EXPERTS, 2, SLOTS, FF), 1.0, 6.0, ((0, 4), (2, 2), (3, 4)))
    return dict(out_grad=out_grad, expert_ids=expert_ids, combine_weights=combine_weights, down_weight=down_weight, saved_pre=saved_pre)


def slot_rows(expert_ids):
    blocks = expert_ids.shape[0] // TOK_DEV
    expert_table = expert_ids.reshape(blocks, TOK_DEV, TOP)
    labels = jnp.arange(EXPERTS, dtype=jnp.int32)
    onehot = (expert_table[:, :, :, None] == labels).astype(jnp.int32)
    per_token = jnp.sum(onehot, axis=2, dtype=jnp.int32)
    before = jnp.cumsum(per_token, axis=1, dtype=jnp.int32) - per_token
    position = jnp.sum(onehot * before[:, :, None, :], axis=3, dtype=jnp.int32)
    return expert_table * CAP + position


def expert_grads(routed, weight_row, projection, saved):
    gate_pre = saved[0].astype(jnp.float32)
    up_pre = saved[1].astype(jnp.float32)
    activated = jax.nn.silu(gate_pre)
    hidden = activated * up_pre
    hidden_b = hidden.astype(jnp.bfloat16)
    scaled = (weight_row[:, None] * hidden).astype(jnp.bfloat16)
    back_grad = lax.dot_general(routed, projection, (((1,), (1,)), ((), ())), preferred_element_type=jnp.float32)
    hidden_grad = weight_row[:, None] * back_grad
    sigmoid_gate = jax.nn.sigmoid(gate_pre)
    gate_grad = hidden_grad * up_pre * sigmoid_gate * (1.0 + gate_pre * (1.0 - sigmoid_gate))
    up_grad = hidden_grad * activated
    pre_grad = jnp.stack([gate_grad, up_grad]).astype(jnp.bfloat16)
    expert_out = jnp.dot(hidden_b, projection, preferred_element_type=jnp.float32)
    scores = jnp.sum(routed.astype(jnp.float32) * expert_out, axis=1)
    groups = routed.shape[0] // (EXPERTS * CAP)

    def add_group(running, paired):
        part_h, part_g = paired
        partial_value = lax.dot_general(part_h, part_g, (((0,), (0,)), ((), ())), preferred_element_type=jnp.float32)
        partial_value = lax.optimization_barrier(partial_value.astype(jnp.bfloat16))
        return running + partial_value.astype(jnp.float32), None

    running, _ = lax.scan(add_group, jnp.zeros((FF, D), jnp.float32),
                          (scaled.reshape(groups, -1, FF), routed.reshape(groups, -1, D)))
    return pre_grad, running.astype(jnp.bfloat16), scores


def reference(out_grad, expert_ids, combine_weights, down_weight, saved_pre):
    blocks = out_grad.shape[0] // TOK_DEV
    slot_index = slot_rows(expert_ids)
    block_index = jnp.broadcast_to(jnp.arange(blocks, dtype=jnp.int32)[:, None, None], slot_index.shape)
    token_rows = jnp.broadcast_to(out_grad.reshape(blocks, TOK_DEV, 1, D), (blocks, TOK_DEV, TOP, D))
    routed = jnp.zeros((blocks, EXPERTS * CAP, D), out_grad.dtype).at[block_index, slot_index].set(token_rows)
    weights = lax.optimization_barrier(combine_weights.astype(jnp.bfloat16))
    weights = weights.astype(jnp.float32).reshape(blocks, TOK_DEV, TOP)
    routed_weight = jnp.zeros((blocks, EXPERTS * CAP), jnp.float32).at[block_index, slot_index].set(weights)
    routed_e = routed.reshape(blocks, EXPERTS, CAP, D).transpose(1, 0, 2, 3).reshape(EXPERTS, blocks * CAP, D)
    weight_e = routed_weight.reshape(blocks, EXPERTS, CAP).transpose(1, 0, 2).reshape(EXPERTS, blocks * CAP)

    def per_expert(packed):
        return expert_grads(packed[0], packed[1], packed[2], packed[3])

    pre_grad, w_grad, scores = lax.map(per_expert, (routed_e, weight_e, down_weight, saved_pre))
    score_blocks = scores.reshape(EXPERTS, blocks, CAP).transpose(1, 0, 2).reshape(blocks, EXPERTS * CAP)
    prob_grad = jnp.take_along_axis(score_blocks, slot_index.reshape(blocks, TOK_DEV * TOP), axis=1)
    return pre_grad, w_grad, prob_grad.reshape(blocks * TOK_DEV, TOP)
```

```python
import functools
import jax
import jax.numpy as jnp
from jax import lax
from jax.experimental import pallas as pl
from jax.experimental.pallas import tpu as pltpu
from jax.sharding import PartitionSpec as P

MESH = pl.DeviceIdType.MESH


def gather_kernel(dims, own_ref, meta_ref, raw_ref, oth_ref, metas_ref,
                  zs, zr, es, er, xs, xr, ms, mr, loc):
    dp, n, experts, cpd = dims
    d, p, e = lax.axis_index("dp"), lax.axis_index("pipe"), lax.axis_index("expert")
    group = dp * experts
    me = d * experts + e
    has_up, has_down = p < n - 1, p > 0
    masks = []
    m = experts // 2
    while m:
        masks.append(m)
        m //= 2

    def flip(value, mask):
        return value + mask * (1 - 2 * (lax.rem(value // mask, 2)))

    def peer(k):
        t = lax.rem(me + k, group)
        return {"dp": t // experts, "pipe": p, "expert": lax.rem(t, experts)}

    def source(k):
        return lax.rem(me + group - k, group)

    barrier = pltpu.get_barrier_semaphore()

    def greet(k, c):
        pl.semaphore_signal(barrier, inc=1, device_id=peer(k), device_id_type=MESH)
        return c

    lax.fori_loop(1, group, greet, 0)

    @pl.when(has_up)
    def _():
        pl.semaphore_signal(barrier, inc=1, device_id={"dp": d, "pipe": p + 1, "expert": e}, device_id_type=MESH)

    @pl.when(has_down)
    def _():
        pl.semaphore_signal(barrier, inc=1, device_id={"dp": d, "pipe": p - 1, "expert": e}, device_id_type=MESH)

    pl.semaphore_wait(barrier, group - 1 + has_up.astype(jnp.int32) + has_down.astype(jnp.int32))

    def meta_copy(k, slot):
        return pltpu.make_async_remote_copy(
            src_ref=meta_ref, dst_ref=metas_ref.at[slot], send_sem=ms.at[k], recv_sem=mr.at[k],
            device_id=peer(k), device_id_type=MESH)

    def z_copy(src, q, s, where):
        return pltpu.make_async_remote_copy(
            src_ref=src, dst_ref=raw_ref.at[q, e], send_sem=zs.at[where, s], recv_sem=zr.at[where, s],
            device_id={"dp": d, "pipe": p + (1 if where == 0 else -1), "expert": e}, device_id_type=MESH)

    def unit_view(unit, b):
        kind, i = unit
        if kind == "own":
            return raw_ref.at[i, b]
        return oth_ref.at[kind, i, b]

    def unit_sem(unit):
        kind, i = unit
        return i if kind == "own" else n + kind * cpd + i

    def e_copy(unit, phase, i, src=None):
        block = e
        for j in range(phase):
            if (i // (1 << j)) % 2:
                block = flip(block, masks[j])
        k = (1 << phase) - 1 + i
        u = unit_sem(unit)
        view = unit_view(unit, block)
        return pltpu.make_async_remote_copy(
            src_ref=view if src is None else src, dst_ref=view, send_sem=es.at[u, k], recv_sem=er.at[u, k],
            device_id={"dp": d, "pipe": p, "expert": flip(e, masks[phase])}, device_id_type=MESH)

    def first(unit, src=None):
        for phase in range(len(masks)):
            e_copy(unit, phase, 0, src).start()

    def rest(unit):
        for phase in range(len(masks)):
            for i in range(1 << phase):
                e_copy(unit, phase, i).wait_recv()
                arrived = i + (1 << phase)
                for later in range(phase + 1, len(masks)):
                    e_copy(unit, later, arrived).start()

    def drain(unit):
        for phase in range(len(masks)):
            for i in range(1 << phase):
                e_copy(unit, phase, i).wait_send()

    def x_copy(k, q, src):
        o = lax.rem(d + k, dp)
        i = q - o * cpd
        return o, pltpu.make_async_remote_copy(
            src_ref=src, dst_ref=oth_ref.at[k - 1, i, e], send_sem=xs.at[k - 1, i], recv_sem=xr.at[k - 1, i],
            device_id={"dp": o, "pipe": p, "expert": e}, device_id_type=MESH)

    def x_send(q, src):
        for k in range(1, dp):
            o = lax.rem(d + k, dp)

            @pl.when(q // cpd == o)
            def _():
                x_copy(k, q, src)[1].start()

    @pl.when(has_up)
    def _():
        z_copy(own_ref, p, 0, 0).start()

    @pl.when(has_down)
    def _():
        z_copy(own_ref, p, 0, 1).start()

    first(("own", p), own_ref)
    x_send(p, own_ref)

    def metas(k, c):
        meta_copy(k, me).start()
        return c

    lax.fori_loop(1, group, metas, 0)
    local = pltpu.make_async_copy(own_ref, raw_ref.at[p, e], loc.at[0])
    local.start()
    local_meta = pltpu.make_async_copy(meta_ref, metas_ref.at[me], loc.at[1])
    local_meta.start()

    for s in range(1, n):
        @pl.when(p - s >= 0)
        def _():
            q = p - s
            z_copy(raw_ref.at[q, e], q, s - 1, 0).wait_recv()

            @pl.when(has_up)
            def _():
                z_copy(raw_ref.at[q, e], q, s, 0).start()

            first(("own", q))
            x_send(q, raw_ref.at[q, e])

        @pl.when(p + s < n)
        def _():
            q = p + s
            z_copy(raw_ref.at[q, e], q, s - 1, 1).wait_recv()

            @pl.when(has_down)
            def _():
                z_copy(raw_ref.at[q, e], q, s, 1).start()

            first(("own", q))
            x_send(q, raw_ref.at[q, e])

    rest(("own", p))
    for s in range(1, n):
        @pl.when(p - s >= 0)
        def _():
            rest(("own", p - s))

        @pl.when(p + s < n)
        def _():
            rest(("own", p + s))

    others = [(k - 1, i) for k in range(1, dp) for i in range(cpd)]
    for kind, i in others:
        pltpu.make_async_remote_copy(
            src_ref=oth_ref.at[kind, i, e], dst_ref=oth_ref.at[kind, i, e], send_sem=xs.at[kind, i],
            recv_sem=xr.at[kind, i], device_id={"dp": lax.rem(d + kind + 1, dp), "pipe": p, "expert": e},
            device_id_type=MESH).wait_recv()
        first((kind, i))
    for unit in others:
        rest(unit)

    for q in range(n):
        drain(("own", q))
    for unit in others:
        drain(unit)
        x_copy(unit[0] + 1, lax.rem(d + unit[0] + 1, dp) * cpd + unit[1], own_ref)[1].wait_send()
    for s in range(n):
        @pl.when((p - s >= 0) & has_up)
        def _():
            z_copy(own_ref, p - s, s, 0).wait_send()

        @pl.when((p + s < n) & has_down)
        def _():
            z_copy(own_ref, p + s, s, 1).wait_send()

    def metas_done(k, c):
        meta_copy(k, me).wait_send()
        meta_copy(k, source(k)).wait_recv()
        return c

    lax.fori_loop(1, group, metas_done, 0)
    local.wait()
    local_meta.wait()


def gather(own, meta, dp, n, experts):
    tokens, cw = own.shape
    cpd = n // dp
    group = dp * experts
    vm = pl.BlockSpec(memory_space=pltpu.VMEM)
    units = n + (dp - 1) * cpd
    dma = pltpu.SemaphoreType.DMA
    return pl.pallas_call(
        functools.partial(gather_kernel, (dp, n, experts, cpd)),
        out_shape=(
            jax.ShapeDtypeStruct((n, experts, tokens, cw), own.dtype),
            jax.ShapeDtypeStruct((dp - 1, cpd, experts, tokens, cw), own.dtype),
            jax.ShapeDtypeStruct((group,) + meta.shape, meta.dtype),
        ),
        in_specs=[vm, vm],
        out_specs=(vm, vm, vm),
        scratch_shapes=[
            dma((2, n)), dma((2, n)),
            dma((units, experts - 1)), dma((units, experts - 1)),
            dma((dp - 1, cpd)), dma((dp - 1, cpd)),
            dma((group,)), dma((group,)), dma((2,)),
        ],
        compiler_params=pltpu.CompilerParams(
            collective_id=0, has_side_effects=True, vmem_limit_bytes=48 * 1024 * 1024),
        cost_estimate=pl.CostEstimate(flops=40_000_000_000, bytes_accessed=60_000_000, transcendentals=0),
    )(own, meta)


def body(out_grad, expert_ids, combine_weights, down_weight, saved_pre):
    experts, dp, n = lax.axis_size("expert"), lax.axis_size("dp"), lax.axis_size("pipe")
    e, d = lax.axis_index("expert"), lax.axis_index("dp")
    slot_count = saved_pre.shape[2]
    capacity = slot_count // experts
    tokens = out_grad.shape[0]

    gate_pre = saved_pre[0, 0].astype(jnp.float32)
    up_pre = saved_pre[0, 1].astype(jnp.float32)
    sigmoid_gate = jax.nn.sigmoid(gate_pre)
    activated = gate_pre * sigmoid_gate
    hidden_b = (activated * up_pre).astype(jnp.bfloat16)
    hidden_all = [hidden_b]
    for k in range(1, dp):
        hidden_all.append(lax.ppermute(hidden_b, "dp", [(i, (i + k) % dp) for i in range(dp)]))

    labels = jnp.arange(experts, dtype=jnp.int32)
    hit = expert_ids.T[None, :, :] == labels[:, None, None]
    named = jnp.any(hit, axis=1)
    earlier = jnp.arange(tokens)[:, None] < jnp.arange(tokens)[None, :]
    position = jnp.dot(named.astype(jnp.bfloat16), earlier.astype(jnp.bfloat16),
                       preferred_element_type=jnp.float32)
    position = jnp.where(named, position, -1.0)
    rounded = lax.optimization_barrier(combine_weights.astype(jnp.bfloat16)).astype(jnp.float32)
    weight = jnp.sum(jnp.where(hit, rounded.T[None], 0.0), axis=1)
    meta = jnp.concatenate([position, weight], axis=0)

    raw, oth, metas = gather(out_grad, meta, dp, n, experts)

    metas = metas.reshape(dp, experts, 2 * experts, tokens)
    where_all = lax.dynamic_index_in_dim(metas, e, 2, keepdims=False)
    weight_all = lax.dynamic_index_in_dim(metas, experts + e, 2, keepdims=False)
    slots = jnp.arange(capacity, dtype=jnp.float32)

    def pick(k):
        at = lax.rem(d - k + dp, dp)
        where = lax.dynamic_index_in_dim(where_all, at, 0, keepdims=False)
        wt = lax.dynamic_index_in_dim(weight_all, at, 0, keepdims=False)
        chosen = where[:, None, :] == slots[None, :, None]
        return chosen, jnp.where(chosen, wt[:, None, :], 0.0)

    def route(sel, data):
        out = lax.dot_general(sel.astype(jnp.bfloat16), data, (((2,), (2,)), ((0,), (1,))),
                              preferred_element_type=jnp.float32)
        return out.astype(jnp.bfloat16).reshape(slot_count, -1)

    chosen, weighted = pick(0)
    weight_row = jnp.sum(weighted, axis=2).reshape(slot_count)
    segment = route(chosen, raw)
    cpd = n // dp
    mine = lax.dynamic_slice_in_dim(raw, d * cpd, cpd, 0)
    segs = [route(weighted, mine)]
    for k in range(1, dp):
        segs.append(route(pick(k)[1], oth[k - 1]))

    back_grad = lax.dot_general(segment, down_weight[0], (((1,), (1,)), ((), ())),
                                preferred_element_type=jnp.float32)
    scores = jnp.sum(hidden_b.astype(jnp.float32) * back_grad, axis=1)
    hidden_grad = weight_row[:, None] * back_grad
    gate_grad = hidden_grad * up_pre * sigmoid_gate * (1.0 + gate_pre * (1.0 - sigmoid_gate))
    up_grad = hidden_grad * activated
    pre_grad = jnp.stack([gate_grad, up_grad]).astype(jnp.bfloat16)[None]

    total = scores.reshape(experts, capacity)
    part = total
    for k in range(1, n):
        total = total + lax.ppermute(part, "pipe", [(i, (i + k) % n) for i in range(n)])
    returned = lax.dynamic_update_slice_in_dim(
        jnp.zeros_like(total), lax.dynamic_slice_in_dim(total, e, 1, 0), e, 0)
    for k in range(1, experts):
        block = lax.dynamic_slice_in_dim(total, lax.rem(e + k, experts), 1, 0)
        got = lax.ppermute(block, "expert", [(i, (i + k) % experts) for i in range(experts)])
        returned = lax.dynamic_update_slice_in_dim(returned, got, lax.rem(e - k + experts, experts), 0)
    place = position[:, :, None] == slots[None, None, :]
    by_expert = jnp.sum(jnp.where(place, returned[:, None, :], 0.0), axis=2)
    prob_grad = jnp.sum(jnp.where(hit, by_expert[:, None, :], 0.0), axis=0).T

    w_grad = lax.dot_general(
        jnp.concatenate(hidden_all, axis=0), jnp.concatenate(segs, axis=0),
        (((0,), (0,)), ((), ())), preferred_element_type=jnp.float32).astype(jnp.bfloat16)
    return (pre_grad, w_grad[None], prob_grad)


def solution(mesh):
    in_specs = (
        P(("dp", "expert"), "pipe"),
        P(("dp", "expert"), None),
        P(("dp", "expert"), None),
        P("expert", "pipe", None),
        P("expert", None, "dp", "pipe"),
    )
    out_specs = (
        P("expert", None, "dp", "pipe"),
        P("expert", "pipe", "dp"),
        P(("dp", "expert"), None),
    )
    return jax.shard_map(body, mesh=mesh, in_specs=in_specs, out_specs=out_specs, check_vma=False)
```

```python
import functools
import jax
import jax.numpy as jnp
from jax import lax
from jax.experimental import pallas as pl
from jax.experimental.pallas import tpu as pltpu
from jax.sharding import PartitionSpec as P

MESH = pl.DeviceIdType.MESH


PIECES = 4


def gather_kernel(dims, own_ref, meta_ref, hidden_ref, weight_hbm,
                  back_ref, segw_ref, hid_ref, metas_ref,
                  raw_ref, oth_ref, w_ref, sel_ref, wsel_ref, seg_ref,
                  zs, zr, es, er, xs, xr, ms, mr, hs, hr, ws, loc):
    dp, n, experts, cpd = dims
    d, p, e = lax.axis_index("dp"), lax.axis_index("pipe"), lax.axis_index("expert")
    tokens, cw = own_ref.shape
    slot_count, width = hidden_ref.shape
    capacity = slot_count // experts
    rows = slot_count // PIECES
    tile = 256 if width % 256 == 0 else width
    group = dp * experts
    me = d * experts + e
    has_up, has_down = p < n - 1, p > 0
    masks = []
    m = experts // 2
    while m:
        masks.append(m)
        m //= 2

    def flip(value, mask):
        return value + mask * (1 - 2 * (lax.rem(value // mask, 2)))

    def peer(k):
        t = lax.rem(me + k, group)
        return {"dp": t // experts, "pipe": p, "expert": lax.rem(t, experts)}

    def source(k):
        return lax.rem(me + group - k, group)

    lo, hi = p, n - 1 - p
    both = jnp.where(lo < hi, lo, hi)

    def chunk(a):
        near = jnp.where(lax.rem(a, 2) == 1, p - (a + 1) // 2, p + a // 2)
        far = jnp.where(lo > hi, p - (a - both), p + (a - both))
        return jnp.where(a <= 2 * both, near, far)

    def w_copy(a):
        q = chunk(a)
        return pltpu.make_async_copy(
            weight_hbm.at[:, pl.ds(pl.multiple_of(q * cw, cw), cw)], w_ref.at[q], ws.at[q])

    local = pltpu.make_async_copy(own_ref, raw_ref.at[p, e], loc.at[0])
    local.start()
    local_meta = pltpu.make_async_copy(meta_ref, metas_ref.at[me], loc.at[1])
    local_meta.start()
    local_hidden = pltpu.make_async_copy(hidden_ref, hid_ref.at[0], loc.at[2])
    local_hidden.start()

    barrier = pltpu.get_barrier_semaphore()

    def greet(k, c):
        pl.semaphore_signal(barrier, inc=1, device_id=peer(k), device_id_type=MESH)
        return c

    lax.fori_loop(1, group, greet, 0)

    @pl.when(has_up)
    def _():
        pl.semaphore_signal(barrier, inc=1, device_id={"dp": d, "pipe": p + 1, "expert": e}, device_id_type=MESH)

    @pl.when(has_down)
    def _():
        pl.semaphore_signal(barrier, inc=1, device_id={"dp": d, "pipe": p - 1, "expert": e}, device_id_type=MESH)

    pl.semaphore_wait(barrier, group - 1 + has_up.astype(jnp.int32) + has_down.astype(jnp.int32))

    def meta_copy(k, slot):
        return pltpu.make_async_remote_copy(
            src_ref=meta_ref, dst_ref=metas_ref.at[slot], send_sem=ms.at[k], recv_sem=mr.at[k],
            device_id=peer(k), device_id_type=MESH)

    def z_copy(src, q, s, where):
        return pltpu.make_async_remote_copy(
            src_ref=src, dst_ref=raw_ref.at[q, e], send_sem=zs.at[where, s], recv_sem=zr.at[where, s],
            device_id={"dp": d, "pipe": p + 1 - 2 * where, "expert": e}, device_id_type=MESH)

    def e_copy(ref, i, u, phase, step, src=None):
        block = e
        for j in range(phase):
            if (step // (1 << j)) % 2:
                block = flip(block, masks[j])
        k = (1 << phase) - 1 + step
        view = ref.at[i, block]
        return pltpu.make_async_remote_copy(
            src_ref=view if src is None else src, dst_ref=view, send_sem=es.at[u, k], recv_sem=er.at[u, k],
            device_id={"dp": d, "pipe": p, "expert": flip(e, masks[phase])}, device_id_type=MESH)

    def first(ref, i, u, src=None):
        for phase in range(len(masks)):
            e_copy(ref, i, u, phase, 0, src).start()

    def rest(ref, i, u):
        for phase in range(len(masks)):
            for step in range(1 << phase):
                e_copy(ref, i, u, phase, step).wait_recv()
                arrived = step + (1 << phase)
                for later in range(phase + 1, len(masks)):
                    e_copy(ref, i, u, later, arrived).start()

    def drain(ref, i, u):
        for phase in range(len(masks)):
            for step in range(1 << phase):
                e_copy(ref, i, u, phase, step).wait_send()

    def x_copy(k, i, src):
        return pltpu.make_async_remote_copy(
            src_ref=src, dst_ref=oth_ref.at[(k - 1) * cpd + i, e], send_sem=xs.at[k - 1, i],
            recv_sem=xr.at[k - 1, i],
            device_id={"dp": lax.rem(d + k, dp), "pipe": p, "expert": e}, device_id_type=MESH)

    def x_send(q, src):
        for k in range(1, dp):
            o = lax.rem(d + k, dp)

            @pl.when(q // cpd == o)
            def _():
                x_copy(k, q - o * cpd, src).start()

    def h_copy(k, r):
        span = pl.ds(pl.multiple_of(r * rows, 16), rows)
        return pltpu.make_async_remote_copy(
            src_ref=hidden_ref.at[span, :], dst_ref=hid_ref.at[k, span, :],
            send_sem=hs.at[k - 1, r], recv_sem=hr.at[k - 1, r],
            device_id={"dp": lax.rem(d + k, dp), "pipe": p, "expert": e}, device_id_type=MESH)

    def h_send(r):
        for k in range(1, dp):
            h_copy(k, r).start()

    def metas(k, c):
        meta_copy(k, me).start()
        return c

    lax.fori_loop(1, group, metas, 0)

    @pl.when(has_up)
    def _():
        z_copy(own_ref, p, 0, 0).start()

    @pl.when(has_down)
    def _():
        z_copy(own_ref, p, 0, 1).start()

    first(raw_ref, p, p, own_ref)
    x_send(p, own_ref)
    h_send(0)

    def w_start(a, c):
        w_copy(a).start()
        return c

    lax.fori_loop(0, n, w_start, 0)
    back_ref[...] = jnp.zeros_like(back_ref)

    def metas_done(k, c):
        meta_copy(k, me).wait_send()
        meta_copy(k, source(k)).wait_recv()
        return c

    local_meta.wait()
    lax.fori_loop(1, group, metas_done, 0)
    local.wait()

    slot = lax.broadcasted_iota(jnp.int32, (slot_count, tokens), 0).astype(jnp.float32)

    def build(k, c):
        at = lax.rem(d - k + dp, dp)
        for b in range(experts):
            where = metas_ref[at * experts + b, pl.ds(e, 1), :]
            weight = metas_ref[at * experts + b, pl.ds(experts + e, 1), :]
            chosen = jnp.where(where >= 0.0, where + float(b * capacity), -1.0) == slot
            wsel_ref[k, :, b * tokens:(b + 1) * tokens] = jnp.where(chosen, weight, 0.0).astype(jnp.bfloat16)

            @pl.when(k == 0)
            def _():
                sel_ref[:, b * tokens:(b + 1) * tokens] = jnp.where(chosen, 1.0, 0.0).astype(jnp.bfloat16)
        return c

    lax.fori_loop(0, dp, build, 0)

    def weigh(k, i, data):
        out = jnp.dot(wsel_ref[k], data, preferred_element_type=jnp.float32)
        segw_ref[k, :, pl.ds(pl.multiple_of(i * cw, cw), cw)] = out.astype(jnp.bfloat16)

    def compute(a):
        q = chunk(a)
        rest(raw_ref, q, q)
        data = raw_ref[q].reshape(experts * tokens, cw)
        seg_ref[...] = jnp.dot(sel_ref[...], data, preferred_element_type=jnp.float32).astype(jnp.bfloat16)

        @pl.when(q // cpd == d)
        def _():
            weigh(0, q - d * cpd, data)

        w_copy(a).wait()

        def part(t, c):
            at = pl.multiple_of(t * tile, tile)
            back_ref[:, pl.ds(at, tile)] += lax.dot_general(
                seg_ref[...], w_ref[q, pl.ds(at, tile), :], (((1,), (1,)), ((), ())),
                preferred_element_type=jnp.float32)
            return c

        lax.fori_loop(0, width // tile, part, 0)

    def advance(a, c):
        q = chunk(a)
        below = q < p
        where = jnp.where(below, 0, 1)
        s = jnp.where(below, p - q, q - p)
        z_copy(raw_ref.at[q, e], q, s - 1, where).wait_recv()

        @pl.when((below & has_up) | ((q > p) & has_down))
        def _():
            z_copy(raw_ref.at[q, e], q, s, where).start()

        first(raw_ref, q, q)
        x_send(q, raw_ref.at[q, e])

        @pl.when(a < PIECES)
        def _():
            h_send(a)

        compute(a - 1)
        return c

    lax.fori_loop(1, n, advance, 0)
    reverse = p > d * cpd
    others = (dp - 1) * cpd

    def turn(u):
        i = lax.rem(u, cpd)
        return u // cpd, jnp.where(reverse, cpd - 1 - i, i)

    def x_arrive(u, c):
        kind, i = turn(u)
        x_copy(kind + 1, i, oth_ref.at[kind * cpd + i, e]).wait_recv()
        first(oth_ref, kind * cpd + i, n + kind * cpd + i)
        return c

    compute(n - 1)
    lax.fori_loop(0, others, x_arrive, 0)

    def x_finish(u, c):
        kind, i = turn(u)
        rest(oth_ref, kind * cpd + i, n + kind * cpd + i)
        weigh(kind + 1, i, oth_ref[kind * cpd + i].reshape(experts * tokens, cw))
        return c

    lax.fori_loop(0, others, x_finish, 0)

    def own_drain(q, c):
        drain(raw_ref, q, q)
        return c

    lax.fori_loop(0, n, own_drain, 0)

    def oth_drain(u, c):
        kind, i = u // cpd, lax.rem(u, cpd)
        drain(oth_ref, u, n + u)
        x_copy(kind + 1, i, own_ref).wait_send()
        return c

    lax.fori_loop(0, others, oth_drain, 0)

    def z_drain(s, c):
        @pl.when((p - s >= 0) & has_up)
        def _():
            z_copy(own_ref, p - s, s, 0).wait_send()

        @pl.when((p + s < n) & has_down)
        def _():
            z_copy(own_ref, p + s, s, 1).wait_send()

        return c

    lax.fori_loop(0, n, z_drain, 0)
    for k in range(1, dp):
        for r in range(PIECES):
            h_copy(k, r).wait()
    local_hidden.wait()


def gather(own, meta, hidden, weight, dp, n, experts):
    tokens, cw = own.shape
    slot_count, width = hidden.shape
    cpd = n // dp
    group = dp * experts
    vm = pl.BlockSpec(memory_space=pltpu.VMEM)
    units = n + (dp - 1) * cpd
    dma = pltpu.SemaphoreType.DMA
    return pl.pallas_call(
        functools.partial(gather_kernel, (dp, n, experts, cpd)),
        out_shape=(
            jax.ShapeDtypeStruct((slot_count, width), jnp.float32),
            jax.ShapeDtypeStruct((dp, slot_count, cpd * cw), own.dtype),
            jax.ShapeDtypeStruct((dp, slot_count, width), hidden.dtype),
            jax.ShapeDtypeStruct((group,) + meta.shape, meta.dtype),
        ),
        in_specs=[vm, vm, vm, pl.BlockSpec(memory_space=pl.ANY)],
        out_specs=(vm, vm, vm, vm),
        scratch_shapes=[
            pltpu.VMEM((n, experts, tokens, cw), own.dtype),
            pltpu.VMEM(((dp - 1) * cpd, experts, tokens, cw), own.dtype),
            pltpu.VMEM((n, width, cw), weight.dtype),
            pltpu.VMEM((slot_count, experts * tokens), jnp.bfloat16),
            pltpu.VMEM((dp, slot_count, experts * tokens), jnp.bfloat16),
            pltpu.VMEM((slot_count, cw), jnp.bfloat16),
            dma((2, n)), dma((2, n)),
            dma((units, experts - 1)), dma((units, experts - 1)),
            dma((dp - 1, cpd)), dma((dp - 1, cpd)),
            dma((group,)), dma((group,)),
            dma((dp - 1, PIECES)), dma((dp - 1, PIECES)),
            dma((n,)), dma((3,)),
        ],
        compiler_params=pltpu.CompilerParams(
            collective_id=0, has_side_effects=True, vmem_limit_bytes=56 * 1024 * 1024),
    )(own, meta, hidden, weight)


def body(out_grad, expert_ids, combine_weights, down_weight, saved_pre):
    experts, dp, n = lax.axis_size("expert"), lax.axis_size("dp"), lax.axis_size("pipe")
    e, d = lax.axis_index("expert"), lax.axis_index("dp")
    slot_count = saved_pre.shape[2]
    capacity = slot_count // experts
    tokens = out_grad.shape[0]

    gate_pre = saved_pre[0, 0].astype(jnp.float32)
    up_pre = saved_pre[0, 1].astype(jnp.float32)
    sigmoid_gate = jax.nn.sigmoid(gate_pre)
    activated = gate_pre * sigmoid_gate
    hidden_b = (activated * up_pre).astype(jnp.bfloat16)

    labels = jnp.arange(experts, dtype=jnp.int32)
    hit = expert_ids.T[None, :, :] == labels[:, None, None]
    named = jnp.any(hit, axis=1)
    earlier = jnp.arange(tokens)[:, None] < jnp.arange(tokens)[None, :]
    position = jnp.dot(named.astype(jnp.bfloat16), earlier.astype(jnp.bfloat16),
                       preferred_element_type=jnp.float32)
    position = jnp.where(named, position, -1.0)
    rounded = lax.optimization_barrier(combine_weights.astype(jnp.bfloat16)).astype(jnp.float32)
    weight = jnp.sum(jnp.where(hit, rounded.T[None], 0.0), axis=1)
    meta = jnp.concatenate([position, weight], axis=0)

    back_grad, segw, hidden_all, metas = gather(
        out_grad, meta, hidden_b, down_weight[0], dp, n, experts)

    metas = metas.reshape(dp, experts, 2 * experts, tokens)
    own_metas = lax.dynamic_index_in_dim(metas, d, 0, keepdims=False)
    where = lax.dynamic_index_in_dim(own_metas, e, 1, keepdims=False)
    wt = lax.dynamic_index_in_dim(own_metas, experts + e, 1, keepdims=False)
    slots = jnp.arange(capacity, dtype=jnp.float32)
    chosen = where[:, None, :] == slots[None, :, None]
    weight_row = jnp.sum(jnp.where(chosen, wt[:, None, :], 0.0), axis=2).reshape(slot_count)

    scores = jnp.sum(hidden_b.astype(jnp.float32) * back_grad, axis=1)
    hidden_grad = weight_row[:, None] * back_grad
    gate_grad = hidden_grad * up_pre * sigmoid_gate * (1.0 + gate_pre * (1.0 - sigmoid_gate))
    up_grad = hidden_grad * activated
    pre_grad = jnp.stack([gate_grad, up_grad]).astype(jnp.bfloat16)[None]

    total = scores.reshape(experts, capacity)
    part = total
    for k in range(1, n):
        total = total + lax.ppermute(part, "pipe", [(i, (i + k) % n) for i in range(n)])
    returned = lax.dynamic_update_slice_in_dim(
        jnp.zeros_like(total), lax.dynamic_slice_in_dim(total, e, 1, 0), e, 0)
    for k in range(1, experts):
        block = lax.dynamic_slice_in_dim(total, lax.rem(e + k, experts), 1, 0)
        got = lax.ppermute(block, "expert", [(i, (i + k) % experts) for i in range(experts)])
        returned = lax.dynamic_update_slice_in_dim(returned, got, lax.rem(e - k + experts, experts), 0)
    place = position[:, :, None] == slots[None, None, :]
    by_expert = jnp.sum(jnp.where(place, returned[:, None, :], 0.0), axis=2)
    prob_grad = jnp.sum(jnp.where(hit, by_expert[:, None, :], 0.0), axis=0).T

    w_grad = lax.dot_general(
        hidden_all.reshape(dp * slot_count, -1), segw.reshape(dp * slot_count, -1),
        (((0,), (0,)), ((), ())), preferred_element_type=jnp.float32).astype(jnp.bfloat16)
    return (pre_grad, w_grad[None], prob_grad)


def solution(mesh):
    in_specs = (
        P(("dp", "expert"), "pipe"),
        P(("dp", "expert"), None),
        P(("dp", "expert"), None),
        P("expert", "pipe", None),
        P("expert", None, "dp", "pipe"),
    )
    out_specs = (
        P("expert", None, "dp", "pipe"),
        P("expert", "pipe", "dp"),
        P(("dp", "expert"), None),
    )
    return jax.shard_map(body, mesh=mesh, in_specs=in_specs, out_specs=out_specs, check_vma=False)
```

```python
import functools
import jax
import jax.numpy as jnp
from jax import lax
from jax.experimental import pallas as pl
from jax.experimental.pallas import tpu as pltpu
from jax.sharding import PartitionSpec as P

MESH = pl.DeviceIdType.MESH


PIECES = 4


def gather_kernel(dims, own_ref, meta_ref, saved_hbm, weight_hbm,
                  pre_ref, segw_ref, hid_ref, score_ref,
                  raw_ref, oth_ref, w_ref, sel_ref, wsel_ref, seg_ref, back_ref, saved_ref, column_ref, metas_ref,
                  zs, zr, es, er, xs, xr, ms, mr, hs, hr, ss, sr, ws, loc):
    dp, n, experts, cpd = dims
    d, p, e = lax.axis_index("dp"), lax.axis_index("pipe"), lax.axis_index("expert")
    tokens, cw = own_ref.shape
    slot_count, width = back_ref.shape
    capacity = slot_count // experts
    rows = slot_count // PIECES
    tile = 256 if width % 256 == 0 else width
    group = dp * experts
    me = d * experts + e
    has_up, has_down = p < n - 1, p > 0
    masks = []
    m = experts // 2
    while m:
        masks.append(m)
        m //= 2

    def flip(value, mask):
        return value + mask * (1 - 2 * (lax.rem(value // mask, 2)))

    def peer(k):
        t = lax.rem(me + k, group)
        return {"dp": t // experts, "pipe": p, "expert": lax.rem(t, experts)}

    def source(k):
        return lax.rem(me + group - k, group)

    lo, hi = p, n - 1 - p
    both = jnp.where(lo < hi, lo, hi)

    def chunk(a):
        near = jnp.where(lax.rem(a, 2) == 1, p - (a + 1) // 2, p + a // 2)
        far = jnp.where(lo > hi, p - (a - both), p + (a - both))
        return jnp.where(a <= 2 * both, near, far)

    def w_copy(a):
        q = chunk(a)
        return pltpu.make_async_copy(
            weight_hbm.at[:, pl.ds(pl.multiple_of(q * cw, cw), cw)], w_ref.at[q], ws.at[q])

    local = pltpu.make_async_copy(own_ref, raw_ref.at[p, e], loc.at[0])
    local.start()
    local_meta = pltpu.make_async_copy(meta_ref, metas_ref.at[me], loc.at[1])
    local_meta.start()
    local_saved = pltpu.make_async_copy(saved_hbm, saved_ref, loc.at[2])
    local_saved.start()

    barrier = pltpu.get_barrier_semaphore()

    def greet(k, c):
        pl.semaphore_signal(barrier, inc=1, device_id=peer(k), device_id_type=MESH)
        return c

    lax.fori_loop(1, group, greet, 0)

    team = n * experts
    mine = p * experts + e

    def mate(k):
        t = lax.rem(mine + k, team)
        return {"dp": d, "pipe": t // experts, "expert": lax.rem(t, experts)}

    def greet_mate(k, c):
        pl.semaphore_signal(barrier, inc=1, device_id=mate(k), device_id_type=MESH)
        return c

    lax.fori_loop(1, team, greet_mate, 0)
    pl.semaphore_wait(barrier, group + team - 2)

    def score_copy(k, slot):
        return pltpu.make_async_remote_copy(
            src_ref=score_ref.at[mine], dst_ref=score_ref.at[slot], send_sem=ss.at[k], recv_sem=sr.at[k],
            device_id=mate(k), device_id_type=MESH)

    def meta_copy(k, slot):
        return pltpu.make_async_remote_copy(
            src_ref=meta_ref, dst_ref=metas_ref.at[slot], send_sem=ms.at[k], recv_sem=mr.at[k],
            device_id=peer(k), device_id_type=MESH)

    def z_copy(src, q, s, where):
        return pltpu.make_async_remote_copy(
            src_ref=src, dst_ref=raw_ref.at[q, e], send_sem=zs.at[where, s], recv_sem=zr.at[where, s],
            device_id={"dp": d, "pipe": p + 1 - 2 * where, "expert": e}, device_id_type=MESH)

    def e_copy(ref, i, u, phase, step, src=None):
        block = e
        for j in range(phase):
            if (step // (1 << j)) % 2:
                block = flip(block, masks[j])
        k = (1 << phase) - 1 + step
        view = ref.at[i, block]
        return pltpu.make_async_remote_copy(
            src_ref=view if src is None else src, dst_ref=view, send_sem=es.at[u, k], recv_sem=er.at[u, k],
            device_id={"dp": d, "pipe": p, "expert": flip(e, masks[phase])}, device_id_type=MESH)

    def first(ref, i, u, src=None):
        for phase in range(len(masks)):
            e_copy(ref, i, u, phase, 0, src).start()

    def rest(ref, i, u):
        for phase in range(len(masks)):
            for step in range(1 << phase):
                e_copy(ref, i, u, phase, step).wait_recv()
                arrived = step + (1 << phase)
                for later in range(phase + 1, len(masks)):
                    e_copy(ref, i, u, later, arrived).start()

    def drain(ref, i, u):
        for phase in range(len(masks)):
            for step in range(1 << phase):
                e_copy(ref, i, u, phase, step).wait_send()

    def x_copy(k, i, src):
        return pltpu.make_async_remote_copy(
            src_ref=src, dst_ref=oth_ref.at[(k - 1) * cpd + i, e], send_sem=xs.at[k - 1, i],
            recv_sem=xr.at[k - 1, i],
            device_id={"dp": lax.rem(d + k, dp), "pipe": p, "expert": e}, device_id_type=MESH)

    def x_send(q, src):
        for k in range(1, dp):
            o = lax.rem(d + k, dp)

            @pl.when(q // cpd == o)
            def _():
                x_copy(k, q - o * cpd, src).start()

    def h_copy(k, r):
        span = pl.ds(pl.multiple_of(r * rows, 16), rows)
        return pltpu.make_async_remote_copy(
            src_ref=hid_ref.at[0, span, :], dst_ref=hid_ref.at[k, span, :],
            send_sem=hs.at[k - 1, r], recv_sem=hr.at[k - 1, r],
            device_id={"dp": lax.rem(d + k, dp), "pipe": p, "expert": e}, device_id_type=MESH)

    def h_send(r):
        for k in range(1, dp):
            h_copy(k, r).start()

    def metas(k, c):
        meta_copy(k, me).start()
        return c

    lax.fori_loop(1, group, metas, 0)

    @pl.when(has_up)
    def _():
        z_copy(own_ref, p, 0, 0).start()

    @pl.when(has_down)
    def _():
        z_copy(own_ref, p, 0, 1).start()

    first(raw_ref, p, p, own_ref)
    x_send(p, own_ref)

    def w_start(a, c):
        w_copy(a).start()
        return c

    lax.fori_loop(0, n, w_start, 0)
    local_saved.wait()
    step_rows = 16

    def pres(t):
        at = pl.ds(pl.multiple_of(t * step_rows, step_rows), step_rows)
        gate = saved_ref[0, at, :].astype(jnp.float32)
        up = saved_ref[1, at, :].astype(jnp.float32)
        sig = jax.nn.sigmoid(gate)
        return at, gate, up, sig, gate * sig

    def make_hidden(t, c):
        at, gate, up, sig, activated = pres(t)
        hid_ref[0, at, :] = (activated * up).astype(jnp.bfloat16)
        return c

    lax.fori_loop(0, slot_count // step_rows, make_hidden, 0)
    back_ref[...] = jnp.zeros_like(back_ref)

    def metas_done(k, c):
        meta_copy(k, me).wait_send()
        meta_copy(k, source(k)).wait_recv()
        return c

    local_meta.wait()
    lax.fori_loop(1, group, metas_done, 0)
    local.wait()

    h_send(0)
    slot = lax.broadcasted_iota(jnp.int32, (slot_count, tokens), 0).astype(jnp.float32)

    def build(k, c):
        at = lax.rem(d - k + dp, dp)
        for b in range(experts):
            where = metas_ref[at * experts + b, pl.ds(e, 1), :]
            weight = metas_ref[at * experts + b, pl.ds(experts + e, 1), :]
            chosen = jnp.where(where >= 0.0, where + float(b * capacity), -1.0) == slot
            wsel_ref[k, :, b * tokens:(b + 1) * tokens] = jnp.where(chosen, weight, 0.0).astype(jnp.bfloat16)

            @pl.when(k == 0)
            def _():
                sel_ref[:, b * tokens:(b + 1) * tokens] = jnp.where(chosen, 1.0, 0.0).astype(jnp.bfloat16)
        return c

    lax.fori_loop(0, dp, build, 0)

    def weigh(k, i, data):
        out = jnp.dot(wsel_ref[k], data, preferred_element_type=jnp.float32)
        segw_ref[k, :, pl.ds(pl.multiple_of(i * cw, cw), cw)] = out.astype(jnp.bfloat16)

    def compute(a):
        q = chunk(a)
        rest(raw_ref, q, q)
        data = raw_ref[q].reshape(experts * tokens, cw)
        seg_ref[...] = jnp.dot(sel_ref[...], data, preferred_element_type=jnp.float32).astype(jnp.bfloat16)

        @pl.when(q // cpd == d)
        def _():
            weigh(0, q - d * cpd, data)

        w_copy(a).wait()

        def part(t, c):
            at = pl.multiple_of(t * tile, tile)
            back_ref[:, pl.ds(at, tile)] += lax.dot_general(
                seg_ref[...], w_ref[q, pl.ds(at, tile), :], (((1,), (1,)), ((), ())),
                preferred_element_type=jnp.float32)
            return c

        lax.fori_loop(0, width // tile, part, 0)

    def arrive(a):
        q = chunk(a)
        below = q < p
        where = jnp.where(below, 0, 1)
        s = jnp.where(below, p - q, q - p)
        z_copy(raw_ref.at[q, e], q, s - 1, where).wait_recv()

        @pl.when((below & has_up) | ((q > p) & has_down))
        def _():
            z_copy(raw_ref.at[q, e], q, s, where).start()

        first(raw_ref, q, q)
        x_send(q, raw_ref.at[q, e])

        @pl.when(a == 1)
        def _():
            h_send(1)

        @pl.when(a == n - 1)
        def _():
            for r in range(2, PIECES):
                h_send(r)

    def advance(a, c):
        arrive(a)
        compute(a - 2)
        return c

    arrive(jnp.int32(1))
    lax.fori_loop(2, n, advance, 0)
    reverse = p > d * cpd
    others = (dp - 1) * cpd

    def turn(u):
        i = lax.rem(u, cpd)
        return u // cpd, jnp.where(reverse, cpd - 1 - i, i)

    def x_arrive(u, c):
        kind, i = turn(u)
        x_copy(kind + 1, i, oth_ref.at[kind * cpd + i, e]).wait_recv()
        first(oth_ref, kind * cpd + i, n + kind * cpd + i)
        return c

    x_arrive(0, 0)
    lax.fori_loop(n - 2, n, lambda a, c: (compute(a), c)[1], 0)

    def finish(t, c):
        at, gate, up, sig, activated = pres(t)
        back = back_ref[at, :]
        score = jnp.sum(hid_ref[0, at, :].astype(jnp.float32) * back, axis=1, keepdims=True)
        column_ref[at, :] = jnp.broadcast_to(score, (step_rows, 128))
        weight_row = jnp.sum(wsel_ref[0, at, :].astype(jnp.float32), axis=1, keepdims=True)
        grad = weight_row * back
        pre_ref[0, at, :] = (grad * up * sig * (1.0 + gate * (1.0 - sig))).astype(jnp.bfloat16)
        pre_ref[1, at, :] = (grad * activated).astype(jnp.bfloat16)
        return c

    column_ref[...] = jnp.zeros_like(column_ref)
    lax.fori_loop(0, slot_count // step_rows, finish, 0)
    score_ref[mine] = jnp.transpose(column_ref[...])[0:8, :]
    lax.fori_loop(1, others, x_arrive, 0)

    def score_send(k, c):
        score_copy(k, mine).start()
        return c

    lax.fori_loop(1, team, score_send, 0)

    def x_finish(u, c):
        kind, i = turn(u)
        rest(oth_ref, kind * cpd + i, n + kind * cpd + i)
        weigh(kind + 1, i, oth_ref[kind * cpd + i].reshape(experts * tokens, cw))
        return c

    lax.fori_loop(0, others, x_finish, 0)

    def own_drain(q, c):
        drain(raw_ref, q, q)
        return c

    lax.fori_loop(0, n, own_drain, 0)

    def oth_drain(u, c):
        kind, i = u // cpd, lax.rem(u, cpd)
        drain(oth_ref, u, n + u)
        x_copy(kind + 1, i, own_ref).wait_send()
        return c

    lax.fori_loop(0, others, oth_drain, 0)

    def z_drain(s, c):
        @pl.when((p - s >= 0) & has_up)
        def _():
            z_copy(own_ref, p - s, s, 0).wait_send()

        @pl.when((p + s < n) & has_down)
        def _():
            z_copy(own_ref, p + s, s, 1).wait_send()

        return c

    lax.fori_loop(0, n, z_drain, 0)
    for k in range(1, dp):
        for r in range(PIECES):
            h_copy(k, r).wait()

    def score_done(k, c):
        score_copy(k, mine).wait_send()
        score_copy(k, lax.rem(mine + team - k, team)).wait_recv()
        return c

    lax.fori_loop(1, team, score_done, 0)


def gather(own, meta, saved, weight, dp, n, experts):
    tokens, cw = own.shape
    _, slot_count, width = saved.shape
    padded = -(-slot_count // 128) * 128
    hbm = pl.BlockSpec(memory_space=pl.ANY)
    cpd = n // dp
    group = dp * experts
    vm = pl.BlockSpec(memory_space=pltpu.VMEM)
    units = n + (dp - 1) * cpd
    dma = pltpu.SemaphoreType.DMA
    return pl.pallas_call(
        functools.partial(gather_kernel, (dp, n, experts, cpd)),
        out_shape=(
            jax.ShapeDtypeStruct((2, slot_count, width), saved.dtype),
            jax.ShapeDtypeStruct((dp, slot_count, cpd * cw), own.dtype),
            jax.ShapeDtypeStruct((dp, slot_count, width), jnp.bfloat16),
            jax.ShapeDtypeStruct((n * experts, 8, padded), jnp.float32),
        ),
        in_specs=[vm, vm, hbm, hbm],
        out_specs=(vm, vm, vm, vm),
        scratch_shapes=[
            pltpu.VMEM((n, experts, tokens, cw), own.dtype),
            pltpu.VMEM(((dp - 1) * cpd, experts, tokens, cw), own.dtype),
            pltpu.VMEM((n, width, cw), weight.dtype),
            pltpu.VMEM((slot_count, experts * tokens), jnp.bfloat16),
            pltpu.VMEM((dp, slot_count, experts * tokens), jnp.bfloat16),
            pltpu.VMEM((slot_count, cw), jnp.bfloat16),
            pltpu.VMEM((slot_count, width), jnp.float32),
            pltpu.VMEM((2, slot_count, width), saved.dtype),
            pltpu.VMEM((padded, 128), jnp.float32),
            pltpu.VMEM((group,) + meta.shape, meta.dtype),
            dma((2, n)), dma((2, n)),
            dma((units, experts - 1)), dma((units, experts - 1)),
            dma((dp - 1, cpd)), dma((dp - 1, cpd)),
            dma((group,)), dma((group,)),
            dma((dp - 1, PIECES)), dma((dp - 1, PIECES)),
            dma((n * experts,)), dma((n * experts,)),
            dma((n,)), dma((3,)),
        ],
        compiler_params=pltpu.CompilerParams(
            collective_id=0, has_side_effects=True, vmem_limit_bytes=56 * 1024 * 1024),
    )(own, meta, saved, weight)


def body(out_grad, expert_ids, combine_weights, down_weight, saved_pre):
    experts, dp, n = lax.axis_size("expert"), lax.axis_size("dp"), lax.axis_size("pipe")
    e = lax.axis_index("expert")
    slot_count = saved_pre.shape[2]
    capacity = slot_count // experts
    tokens = out_grad.shape[0]

    labels = jnp.arange(experts, dtype=jnp.int32)
    hit = expert_ids.T[None, :, :] == labels[:, None, None]
    named = jnp.any(hit, axis=1)
    earlier = jnp.arange(tokens)[:, None] < jnp.arange(tokens)[None, :]
    position = jnp.dot(named.astype(jnp.bfloat16), earlier.astype(jnp.bfloat16),
                       preferred_element_type=jnp.float32)
    position = jnp.where(named, position, -1.0)
    rounded = lax.optimization_barrier(combine_weights.astype(jnp.bfloat16)).astype(jnp.float32)
    weight = jnp.sum(jnp.where(hit, rounded.T[None], 0.0), axis=1)
    meta = jnp.concatenate([position, weight], axis=0)

    pre_grad, segw, hidden_all, scores = gather(
        out_grad, meta, saved_pre[0], down_weight[0], dp, n, experts)
    slots = jnp.arange(capacity, dtype=jnp.float32)
    total = jnp.sum(scores.reshape(n, experts, 8, -1)[:, :, 0, :], axis=0)
    returned = lax.dynamic_slice_in_dim(total, e * capacity, capacity, 1)
    place = position[:, :, None] == slots[None, None, :]
    by_expert = jnp.sum(jnp.where(place, returned[:, None, :], 0.0), axis=2)
    prob_grad = jnp.sum(jnp.where(hit, by_expert[:, None, :], 0.0), axis=0).T

    w_grad = lax.dot_general(
        hidden_all.reshape(dp * slot_count, -1), segw.reshape(dp * slot_count, -1),
        (((0,), (0,)), ((), ())), preferred_element_type=jnp.float32).astype(jnp.bfloat16)
    return (pre_grad[None], w_grad[None], prob_grad)


def solution(mesh):
    in_specs = (
        P(("dp", "expert"), "pipe"),
        P(("dp", "expert"), None),
        P(("dp", "expert"), None),
        P("expert", "pipe", None),
        P("expert", None, "dp", "pipe"),
    )
    out_specs = (
        P("expert", None, "dp", "pipe"),
        P("expert", "pipe", "dp"),
        P(("dp", "expert"), None),
    )
    return jax.shard_map(body, mesh=mesh, in_specs=in_specs, out_specs=out_specs, check_vma=False)
```

```python
import functools
import jax
import jax.numpy as jnp
from jax import lax
from jax.experimental import pallas as pl
from jax.experimental.pallas import tpu as pltpu
from jax.sharding import PartitionSpec as P

MESH = pl.DeviceIdType.MESH


PIECES = 4


def gather_kernel(dims, own_ref, meta_ref, saved_hbm, weight_hbm,
                  pre_ref, segw_ref, hid_ref, score_ref,
                  raw_ref, oth_ref, w_ref, sel_ref, wsel_ref, seg_ref, back_ref, saved_ref, column_ref, metas_ref,
                  zs, zr, es, er, xs, xr, ms, mr, hs, hr, ss, sr, ws, loc):
    dp, n, experts, cpd = dims
    d, p, e = lax.axis_index("dp"), lax.axis_index("pipe"), lax.axis_index("expert")
    tokens, cw = own_ref.shape
    slot_count, width = back_ref.shape
    capacity = slot_count // experts
    rows = slot_count // PIECES
    tile = 256 if width % 256 == 0 else width
    group = dp * experts
    me = d * experts + e
    has_up, has_down = p < n - 1, p > 0
    masks = []
    m = experts // 2
    while m:
        masks.append(m)
        m //= 2

    def flip(value, mask):
        return value + mask * (1 - 2 * (lax.rem(value // mask, 2)))

    def peer(k):
        t = lax.rem(me + k, group)
        return {"dp": t // experts, "pipe": p, "expert": lax.rem(t, experts)}

    def source(k):
        return lax.rem(me + group - k, group)

    lo, hi = p, n - 1 - p
    both = jnp.where(lo < hi, lo, hi)

    def chunk(a):
        near = jnp.where(lax.rem(a, 2) == 1, p - (a + 1) // 2, p + a // 2)
        far = jnp.where(lo > hi, p - (a - both), p + (a - both))
        return jnp.where(a <= 2 * both, near, far)

    def w_copy(a):
        q = chunk(a)
        return pltpu.make_async_copy(
            weight_hbm.at[:, pl.ds(pl.multiple_of(q * cw, cw), cw)], w_ref.at[q], ws.at[q])

    local = pltpu.make_async_copy(own_ref, raw_ref.at[p, e], loc.at[0])
    local.start()
    local_meta = pltpu.make_async_copy(meta_ref, metas_ref.at[me], loc.at[1])
    local_meta.start()
    local_saved = pltpu.make_async_copy(saved_hbm, saved_ref, loc.at[2])
    local_saved.start()

    barrier = pltpu.get_barrier_semaphore()

    def greet(k, c):
        pl.semaphore_signal(barrier, inc=1, device_id=peer(k), device_id_type=MESH)
        return c

    lax.fori_loop(1, group, greet, 0)

    team = n * experts
    mine = p * experts + e

    def mate(k):
        t = lax.rem(mine + k, team)
        return {"dp": d, "pipe": t // experts, "expert": lax.rem(t, experts)}

    def greet_mate(k, c):
        pl.semaphore_signal(barrier, inc=1, device_id=mate(k), device_id_type=MESH)
        return c

    lax.fori_loop(1, team, greet_mate, 0)
    pl.semaphore_wait(barrier, group + team - 2)

    def score_copy(k, slot):
        return pltpu.make_async_remote_copy(
            src_ref=score_ref.at[mine], dst_ref=score_ref.at[slot], send_sem=ss.at[k], recv_sem=sr.at[k],
            device_id=mate(k), device_id_type=MESH)

    def meta_copy(k, slot):
        return pltpu.make_async_remote_copy(
            src_ref=meta_ref, dst_ref=metas_ref.at[slot], send_sem=ms.at[k], recv_sem=mr.at[k],
            device_id=peer(k), device_id_type=MESH)

    half = tokens // 2

    def span(f):
        return pl.ds(f * half, half)

    def z_copy(src, q, s, where, f):
        return pltpu.make_async_remote_copy(
            src_ref=src.at[span(f), :], dst_ref=raw_ref.at[q, e, span(f), :], send_sem=zs.at[where, s, f],
            recv_sem=zr.at[where, s, f],
            device_id={"dp": d, "pipe": p + 1 - 2 * where, "expert": e}, device_id_type=MESH)

    def e_copy(ref, i, u, phase, step, f, src=None):
        block = e
        for j in range(phase):
            if (step // (1 << j)) % 2:
                block = flip(block, masks[j])
        k = (1 << phase) - 1 + step
        view = ref.at[i, block, span(f), :]
        return pltpu.make_async_remote_copy(
            src_ref=view if src is None else src.at[span(f), :], dst_ref=view, send_sem=es.at[u, k, f],
            recv_sem=er.at[u, k, f],
            device_id={"dp": d, "pipe": p, "expert": flip(e, masks[phase])}, device_id_type=MESH)

    def first(ref, i, u, f, src=None):
        for phase in range(len(masks)):
            e_copy(ref, i, u, phase, 0, f, src).start()

    def rest(ref, i, u):
        for phase in range(len(masks)):
            for step in range(1 << phase):
                arrived = step + (1 << phase)
                for f in range(2):
                    e_copy(ref, i, u, phase, step, f).wait_recv()
                    for later in range(phase + 1, len(masks)):
                        e_copy(ref, i, u, later, arrived, f).start()

    def drain(ref, i, u):
        for phase in range(len(masks)):
            for step in range(1 << phase):
                for f in range(2):
                    e_copy(ref, i, u, phase, step, f).wait_send()

    def x_copy(k, i, src, f):
        return pltpu.make_async_remote_copy(
            src_ref=src.at[span(f), :], dst_ref=oth_ref.at[(k - 1) * cpd + i, e, span(f), :],
            send_sem=xs.at[k - 1, i, f], recv_sem=xr.at[k - 1, i, f],
            device_id={"dp": lax.rem(d + k, dp), "pipe": p, "expert": e}, device_id_type=MESH)

    def x_send(q, src, f):
        for k in range(1, dp):
            o = lax.rem(d + k, dp)

            @pl.when(q // cpd == o)
            def _():
                x_copy(k, q - o * cpd, src, f).start()

    def h_copy(k, r):
        part = pl.ds(pl.multiple_of(r * rows, 16), rows)
        return pltpu.make_async_remote_copy(
            src_ref=hid_ref.at[0, part, :], dst_ref=hid_ref.at[k, part, :],
            send_sem=hs.at[k - 1, r], recv_sem=hr.at[k - 1, r],
            device_id={"dp": lax.rem(d + k, dp), "pipe": p, "expert": e}, device_id_type=MESH)

    def h_send(r):
        for k in range(1, dp):
            h_copy(k, r).start()

    def metas(k, c):
        meta_copy(k, me).start()
        return c

    lax.fori_loop(1, group, metas, 0)

    for f in range(2):
        @pl.when(has_up)
        def _():
            z_copy(own_ref, p, 0, 0, f).start()

        @pl.when(has_down)
        def _():
            z_copy(own_ref, p, 0, 1, f).start()

        first(raw_ref, p, p, f, own_ref)
        x_send(p, own_ref, f)

    def w_start(a, c):
        w_copy(a).start()
        return c

    lax.fori_loop(0, n, w_start, 0)
    local_saved.wait()
    step_rows = 16

    def pres(t):
        at = pl.ds(pl.multiple_of(t * step_rows, step_rows), step_rows)
        gate = saved_ref[0, at, :].astype(jnp.float32)
        up = saved_ref[1, at, :].astype(jnp.float32)
        sig = jax.nn.sigmoid(gate)
        return at, gate, up, sig, gate * sig

    def make_hidden(t, c):
        at, gate, up, sig, activated = pres(t)
        hid_ref[0, at, :] = (activated * up).astype(jnp.bfloat16)
        return c

    lax.fori_loop(0, slot_count // step_rows, make_hidden, 0)
    back_ref[...] = jnp.zeros_like(back_ref)

    def metas_done(k, c):
        meta_copy(k, me).wait_send()
        meta_copy(k, source(k)).wait_recv()
        return c

    local_meta.wait()
    lax.fori_loop(1, group, metas_done, 0)
    local.wait()

    h_send(0)
    slot = lax.broadcasted_iota(jnp.int32, (slot_count, tokens), 0).astype(jnp.float32)

    def build(k, c):
        at = lax.rem(d - k + dp, dp)
        for b in range(experts):
            where = metas_ref[at * experts + b, pl.ds(e, 1), :]
            weight = metas_ref[at * experts + b, pl.ds(experts + e, 1), :]
            chosen = jnp.where(where >= 0.0, where + float(b * capacity), -1.0) == slot
            wsel_ref[k, :, b * tokens:(b + 1) * tokens] = jnp.where(chosen, weight, 0.0).astype(jnp.bfloat16)

            @pl.when(k == 0)
            def _():
                sel_ref[:, b * tokens:(b + 1) * tokens] = jnp.where(chosen, 1.0, 0.0).astype(jnp.bfloat16)
        return c

    lax.fori_loop(0, dp, build, 0)

    def weigh(k, i, data):
        out = jnp.dot(wsel_ref[k], data, preferred_element_type=jnp.float32)
        segw_ref[k, :, pl.ds(pl.multiple_of(i * cw, cw), cw)] = out.astype(jnp.bfloat16)

    def compute(a):
        q = chunk(a)
        rest(raw_ref, q, q)
        data = raw_ref[q].reshape(experts * tokens, cw)
        seg_ref[...] = jnp.dot(sel_ref[...], data, preferred_element_type=jnp.float32).astype(jnp.bfloat16)

        @pl.when(q // cpd == d)
        def _():
            weigh(0, q - d * cpd, data)

        w_copy(a).wait()

        def part(t, c):
            at = pl.multiple_of(t * tile, tile)
            back_ref[:, pl.ds(at, tile)] += lax.dot_general(
                seg_ref[...], w_ref[q, pl.ds(at, tile), :], (((1,), (1,)), ((), ())),
                preferred_element_type=jnp.float32)
            return c

        lax.fori_loop(0, width // tile, part, 0)

    def arrive(a):
        q = chunk(a)
        below = q < p
        where = jnp.where(below, 0, 1)
        s = jnp.where(below, p - q, q - p)
        for f in range(2):
            z_copy(raw_ref.at[q, e], q, s - 1, where, f).wait_recv()

            @pl.when((below & has_up) | ((q > p) & has_down))
            def _():
                z_copy(raw_ref.at[q, e], q, s, where, f).start()

            first(raw_ref, q, q, f)
            x_send(q, raw_ref.at[q, e], f)

        @pl.when(a == 1)
        def _():
            h_send(1)

        @pl.when(a == n - 1)
        def _():
            for r in range(2, PIECES):
                h_send(r)

    def advance(a, c):
        arrive(a)
        compute(a - 2)
        return c

    arrive(jnp.int32(1))
    lax.fori_loop(2, n, advance, 0)
    reverse = p > d * cpd
    others = (dp - 1) * cpd

    def turn(u):
        i = lax.rem(u, cpd)
        return u // cpd, jnp.where(reverse, cpd - 1 - i, i)

    def x_arrive(u, c):
        kind, i = turn(u)
        for f in range(2):
            x_copy(kind + 1, i, oth_ref.at[kind * cpd + i, e], f).wait_recv()
            first(oth_ref, kind * cpd + i, n + kind * cpd + i, f)
        return c

    x_arrive(0, 0)
    lax.fori_loop(n - 2, n, lambda a, c: (compute(a), c)[1], 0)

    def finish(t, c):
        at, gate, up, sig, activated = pres(t)
        back = back_ref[at, :]
        score = jnp.sum(hid_ref[0, at, :].astype(jnp.float32) * back, axis=1, keepdims=True)
        column_ref[at, :] = jnp.broadcast_to(score, (step_rows, 128))
        weight_row = jnp.sum(wsel_ref[0, at, :].astype(jnp.float32), axis=1, keepdims=True)
        grad = weight_row * back
        pre_ref[0, at, :] = (grad * up * sig * (1.0 + gate * (1.0 - sig))).astype(jnp.bfloat16)
        pre_ref[1, at, :] = (grad * activated).astype(jnp.bfloat16)
        return c

    column_ref[...] = jnp.zeros_like(column_ref)
    lax.fori_loop(0, slot_count // step_rows, finish, 0)
    score_ref[mine] = jnp.transpose(column_ref[...])[0:8, :]
    lax.fori_loop(1, others, x_arrive, 0)

    def score_send(k, c):
        score_copy(k, mine).start()
        return c

    lax.fori_loop(1, team, score_send, 0)

    def x_finish(u, c):
        kind, i = turn(u)
        rest(oth_ref, kind * cpd + i, n + kind * cpd + i)
        weigh(kind + 1, i, oth_ref[kind * cpd + i].reshape(experts * tokens, cw))
        return c

    lax.fori_loop(0, others, x_finish, 0)

    def own_drain(q, c):
        drain(raw_ref, q, q)
        return c

    lax.fori_loop(0, n, own_drain, 0)

    def oth_drain(u, c):
        kind, i = u // cpd, lax.rem(u, cpd)
        drain(oth_ref, u, n + u)
        for f in range(2):
            x_copy(kind + 1, i, own_ref, f).wait_send()
        return c

    lax.fori_loop(0, others, oth_drain, 0)

    def z_drain(s, c):
        @pl.when((p - s >= 0) & has_up)
        def _():
            for f in range(2):
                z_copy(own_ref, p - s, s, 0, f).wait_send()

        @pl.when((p + s < n) & has_down)
        def _():
            for f in range(2):
                z_copy(own_ref, p + s, s, 1, f).wait_send()

        return c

    lax.fori_loop(0, n, z_drain, 0)
    for k in range(1, dp):
        for r in range(PIECES):
            h_copy(k, r).wait()

    def score_done(k, c):
        score_copy(k, mine).wait_send()
        score_copy(k, lax.rem(mine + team - k, team)).wait_recv()
        return c

    lax.fori_loop(1, team, score_done, 0)


def gather(own, meta, saved, weight, dp, n, experts):
    tokens, cw = own.shape
    _, slot_count, width = saved.shape
    padded = -(-slot_count // 128) * 128
    hbm = pl.BlockSpec(memory_space=pl.ANY)
    cpd = n // dp
    group = dp * experts
    vm = pl.BlockSpec(memory_space=pltpu.VMEM)
    units = n + (dp - 1) * cpd
    dma = pltpu.SemaphoreType.DMA
    return pl.pallas_call(
        functools.partial(gather_kernel, (dp, n, experts, cpd)),
        out_shape=(
            jax.ShapeDtypeStruct((2, slot_count, width), saved.dtype),
            jax.ShapeDtypeStruct((dp, slot_count, cpd * cw), own.dtype),
            jax.ShapeDtypeStruct((dp, slot_count, width), jnp.bfloat16),
            jax.ShapeDtypeStruct((n * experts, 8, padded), jnp.float32),
        ),
        in_specs=[vm, vm, hbm, hbm],
        out_specs=(vm, vm, vm, vm),
        scratch_shapes=[
            pltpu.VMEM((n, experts, tokens, cw), own.dtype),
            pltpu.VMEM(((dp - 1) * cpd, experts, tokens, cw), own.dtype),
            pltpu.VMEM((n, width, cw), weight.dtype),
            pltpu.VMEM((slot_count, experts * tokens), jnp.bfloat16),
            pltpu.VMEM((dp, slot_count, experts * tokens), jnp.bfloat16),
            pltpu.VMEM((slot_count, cw), jnp.bfloat16),
            pltpu.VMEM((slot_count, width), jnp.float32),
            pltpu.VMEM((2, slot_count, width), saved.dtype),
            pltpu.VMEM((padded, 128), jnp.float32),
            pltpu.VMEM((group,) + meta.shape, meta.dtype),
            dma((2, n, 2)), dma((2, n, 2)),
            dma((units, experts - 1, 2)), dma((units, experts - 1, 2)),
            dma((dp - 1, cpd, 2)), dma((dp - 1, cpd, 2)),
            dma((group,)), dma((group,)),
            dma((dp - 1, PIECES)), dma((dp - 1, PIECES)),
            dma((n * experts,)), dma((n * experts,)),
            dma((n,)), dma((3,)),
        ],
        compiler_params=pltpu.CompilerParams(
            collective_id=0, has_side_effects=True, vmem_limit_bytes=56 * 1024 * 1024),
    )(own, meta, saved, weight)


def body(out_grad, expert_ids, combine_weights, down_weight, saved_pre):
    experts, dp, n = lax.axis_size("expert"), lax.axis_size("dp"), lax.axis_size("pipe")
    e = lax.axis_index("expert")
    slot_count = saved_pre.shape[2]
    capacity = slot_count // experts
    tokens = out_grad.shape[0]

    labels = jnp.arange(experts, dtype=jnp.int32)
    hit = expert_ids.T[None, :, :] == labels[:, None, None]
    named = jnp.any(hit, axis=1)
    earlier = jnp.arange(tokens)[:, None] < jnp.arange(tokens)[None, :]
    position = jnp.dot(named.astype(jnp.bfloat16), earlier.astype(jnp.bfloat16),
                       preferred_element_type=jnp.float32)
    position = jnp.where(named, position, -1.0)
    rounded = lax.optimization_barrier(combine_weights.astype(jnp.bfloat16)).astype(jnp.float32)
    weight = jnp.sum(jnp.where(hit, rounded.T[None], 0.0), axis=1)
    meta = jnp.concatenate([position, weight], axis=0)

    pre_grad, segw, hidden_all, scores = gather(
        out_grad, meta, saved_pre[0], down_weight[0], dp, n, experts)
    slots = jnp.arange(capacity, dtype=jnp.float32)
    total = jnp.sum(scores.reshape(n, experts, 8, -1)[:, :, 0, :], axis=0)
    returned = lax.dynamic_slice_in_dim(total, e * capacity, capacity, 1)
    place = position[:, :, None] == slots[None, None, :]
    by_expert = jnp.sum(jnp.where(place, returned[:, None, :], 0.0), axis=2)
    prob_grad = jnp.sum(jnp.where(hit, by_expert[:, None, :], 0.0), axis=0).T

    w_grad = lax.dot_general(
        hidden_all.reshape(dp * slot_count, -1), segw.reshape(dp * slot_count, -1),
        (((0,), (0,)), ((), ())), preferred_element_type=jnp.float32).astype(jnp.bfloat16)
    return (pre_grad[None], w_grad[None], prob_grad)


def solution(mesh):
    in_specs = (
        P(("dp", "expert"), "pipe"),
        P(("dp", "expert"), None),
        P(("dp", "expert"), None),
        P("expert", "pipe", None),
        P("expert", None, "dp", "pipe"),
    )
    out_specs = (
        P("expert", None, "dp", "pipe"),
        P("expert", "pipe", "dp"),
        P(("dp", "expert"), None),
    )
    return jax.shard_map(body, mesh=mesh, in_specs=in_specs, out_specs=out_specs, check_vma=False)
```
